32 devices in a mesh: mesh: 4 (over z), modes: 8 (over y, x, core).
Axes of the slice: x: 2, y: 2, z: 4, core: 2. Of those that a mesh axis runs over, the one named last changes fastest.
Arguments:
- velocity: float32 [3, 128, 81, 512], P(None, 'modes', None, 'mesh'), may hold values from -2 to 2
- metrics: float32 [4, 512], P(None, 'mesh'), as said below
- connect: int32 [512, 4], P('mesh'), may hold values from -1 to 511, as said below
- send_list: int32 [8, 64], P('mesh'), may hold values from 0 to 127, as said below
- recv_slot: int32 [512, 2], P('mesh'), may hold values from -1 to 63, as said below
Outputs:
- new_velocity: float32 [3, 128, 81, 512], P(None, 'modes', None, 'mesh')
- advection: float32 [3, 128, 81, 512], P(None, 'modes', None, 'mesh')
The draws below stay inside these ranges and needn't reach their ends.
Inputs may be any that keep to these rules, and one draw needn't show every extreme that they name: Elements p * 128 to (p + 1) * 128 - 1 form partition p. connect[e, k] is the element across edge k of element e (0 bottom, 1 right, 2 top, 3 left), -1 where that edge is on the cylinder wall or the outer boundary; where recv_slot of that edge is -1 the neighbour lies in e's own partition, and neighbours across edges 1 and 3 always do. Row 2p (row 2p + 1) of send_list names, for each of the 64 edges shared with partition p - 1 (p + 1), the local index within partition p of the element whose bottom (top) edge it is; each row names 64 different elements. recv_slot[e, 0] is the column c such that the bottom neighbour of e is named by send_list[2p - 1, c] of partition p - 1, and -1 where that neighbour is in e's own partition or absent; recv_slot[e, 1] likewise for the top neighbour with send_list[2p + 2, c] of partition p + 1. `metrics`: rows 0 and 3 are positive stretches, rows 1 and 2 smaller shears.
All inputs are finite; a program needn't handle non-finite values.
Results may differ from the reference program's by a relative error of at most 0.0001.
Values sent between devices are 32-bit elements; how exact they have to be, the bound alone decides.
A program may use at most 192 MiB of HBM per device.

```python
import jax
import jax.numpy as jnp
import numpy as np
from jax import lax

COEF = 128
W = 64
RDEV = 2
ITERS = 2
E_DEV = 128
ELEMENTS = 512
N_MESH = 4


def partition_layout(key):
    part_keys = jax.random.split(key, N_MESH)
    slot_cells = jax.vmap(lambda part_key: jax.random.permutation(part_key, E_DEV))(part_keys).astype(jnp.int32)
    inverse = jnp.argsort(slot_cells, axis=1, stable=True).astype(jnp.int32)
    part_ids = jnp.arange(N_MESH, dtype=jnp.int32)[:, None]
    local_row = slot_cells // W
    column = slot_cells % W
    global_row = part_ids * RDEV + local_row
    cycle_count = RDEV * N_MESH

    def locate(cycle_rows, cycle_cols):
        inside = (cycle_rows >= 0) & (cycle_rows < cycle_count)
        clipped = jnp.clip(cycle_rows, 0, cycle_count - 1)
        owner_part = clipped // RDEV
        cell_index = clipped % RDEV * W + cycle_cols
        element_id = owner_part * E_DEV + inverse[owner_part, cell_index]
        return jnp.where(inside, element_id, -1).astype(jnp.int32)
    neighbours = jnp.stack([locate(global_row - 1, column), locate(global_row, (column + 1) % W), locate(global_row + 1, column), locate(global_row, (column + W - 1) % W)], axis=-1)
    connect = neighbours.reshape(ELEMENTS, 4)
    send_rows = jnp.stack([inverse[:, :W], inverse[:, (RDEV - 1) * W:]], axis=1).reshape(2 * N_MESH, W)
    lower_cols = jnp.where((local_row == 0) & (part_ids > 0), column, -1)
    upper_cols = jnp.where((local_row == RDEV - 1) & (part_ids < N_MESH - 1), column, -1)
    receive = jnp.stack([lower_cols, upper_cols], axis=-1).reshape(ELEMENTS, 2).astype(jnp.int32)
    return (connect, send_rows.astype(jnp.int32), receive)


def draw_connect(key, part):
    return partition_layout(jax.random.fold_in(key, 11))[0]


def draw_send_list(key, part):
    return partition_layout(jax.random.fold_in(key, 11))[1]


def draw_recv_slot(key, part):
    return partition_layout(jax.random.fold_in(key, 11))[2]


def draw_metrics(key, part):
    sub_keys = jax.random.split(key, 4)
    stretch_r = jax.random.uniform(sub_keys[0], (ELEMENTS,), jnp.float32, 0.7, 1.3)
    stretch_s = jax.random.uniform(sub_keys[3], (ELEMENTS,), jnp.float32, 0.7, 1.3)
    shear_r = jax.random.uniform(sub_keys[1], (ELEMENTS,), jnp.float32, -0.3, 0.3)
    shear_s = jax.random.uniform(sub_keys[2], (ELEMENTS,), jnp.float32, -0.3, 0.3)
    return jnp.stack([stretch_r, shear_r, shear_s, stretch_s]).astype(jnp.float32)


def block_levels(key, shape, pieces, low, largest):
    level, own = 1.0, jax.random.fold_in(key, 6)
    for dim, blocks in pieces:
        heights = jnp.exp(jax.random.uniform(jax.random.fold_in(own, dim), (blocks,), jnp.float32, low / len(pieces), largest / len(pieces)))
        level = level * jnp.repeat(heights, shape[dim] // blocks).reshape([-1 if axis == dim else 1 for axis in range(len(shape))])
    return level


def normal_values(key, extent, width, limit, cuts=(), kind=jnp.bfloat16):
    drawn = width * jax.random.normal(key, extent, jnp.float32)
    if cuts:
        drawn = drawn * block_levels(key, extent, cuts, -0.22, 0.18)
    return jnp.clip(drawn, -limit, limit).astype(kind)


def setup_inputs(seed: int = 0) -> dict:
    arg_keys = jax.random.split(jax.random.key(seed), 6)
    velocity = normal_values(arg_keys[0], (3, COEF, 81, ELEMENTS), 0.15, 2.0, ((1, 8), (3, 4)), jnp.float32)
    metrics = draw_metrics(jax.random.fold_in(arg_keys[5], 71), 0)
    connect = draw_connect(jax.random.fold_in(arg_keys[5], 71), 0)
    send_list = draw_send_list(jax.random.fold_in(arg_keys[5], 71), 0)
    recv_slot = draw_recv_slot(jax.random.fold_in(arg_keys[5], 71), 0)
    return {"velocity": velocity, "metrics": metrics, "connect": connect, "send_list": send_list, "recv_slot": recv_slot}


highest = lax.Precision.HIGHEST
helm_shift = 4.0
penalty_weight = 200.0
spectral_bound = 400.0
relaxation = 0.8
time_step = 0.02
wave_scale = 0.125
gll_interior = [-0.8997579954114602, -0.6771862795107377, -0.3631174638261782, 0.0, 0.3631174638261782, 0.6771862795107377, 0.8997579954114602]


def legendre_value(point, degree):
    previous = 1.0
    current = point
    for order_index in range(1, degree):
        following = ((2 * order_index + 1) * point * current - order_index * previous) / (order_index + 1)
        previous = current
        current = following
    return current


def spectral_tables(coef_count):
    poly_order = 8
    node_count = poly_order + 1
    points = np.array([-1.0] + gll_interior + [1.0])
    values = np.array([legendre_value(points[node], poly_order) for node in range(node_count)])
    derivative = np.zeros((node_count, node_count))
    for row_index in range(node_count):
        for col_index in range(node_count):
            if row_index != col_index:
                derivative[row_index, col_index] = values[row_index] / (values[col_index] * (points[row_index] - points[col_index]))
    derivative[0, 0] = -poly_order * (poly_order + 1) / 4.0
    derivative[poly_order, poly_order] = poly_order * (poly_order + 1) / 4.0
    identity = np.eye(node_count)
    along_r = np.kron(identity, derivative)
    along_s = np.kron(derivative, identity)
    second = np.stack([along_r @ along_r, along_r @ along_s, along_s @ along_s])
    line_nodes = np.arange(node_count)
    edge_nodes = np.stack([line_nodes, line_nodes * node_count + poly_order, poly_order * node_count + line_nodes, line_nodes * node_count])
    scatter_edge = np.zeros((node_count * node_count, 4 * node_count))
    for edge_index in range(4):
        scatter_edge[edge_nodes[edge_index], edge_index * node_count + line_nodes] = 1.0
    planes = np.arange(coef_count) * 2.0 * np.pi / coef_count
    half_count = coef_count // 2
    wavenumber = np.zeros(coef_count)
    basis = np.zeros((coef_count, coef_count))
    z_derivative = np.zeros((coef_count, coef_count))
    basis[:, 0] = 1.0
    basis[:, 1] = np.cos(half_count * planes)
    wavenumber[1] = half_count
    for mode_number in range(1, half_count):
        basis[:, 2 * mode_number] = np.cos(mode_number * planes)
        basis[:, 2 * mode_number + 1] = np.sin(mode_number * planes)
        wavenumber[2 * mode_number] = mode_number
        wavenumber[2 * mode_number + 1] = mode_number
        z_derivative[2 * mode_number, 2 * mode_number + 1] = wave_scale * mode_number
        z_derivative[2 * mode_number + 1, 2 * mode_number] = -wave_scale * mode_number
    norms = np.full(coef_count, coef_count / 2.0)
    norms[0] = coef_count
    norms[1] = coef_count
    inverse = basis.T / norms[:, None]
    shifts = helm_shift + (wave_scale * wavenumber) ** 2
    plane_derivative = basis @ z_derivative @ inverse
    float_tables = [jnp.asarray(table, dtype=jnp.float32) for table in (along_r, along_s, second, scatter_edge, basis, inverse, z_derivative, shifts, plane_derivative)]
    return float_tables, edge_nodes


def element_factors(metrics):
    return jnp.stack([metrics[0] * metrics[0] + metrics[1] * metrics[1], 2.0 * (metrics[0] * metrics[2] + metrics[1] * metrics[3]), metrics[2] * metrics[2] + metrics[3] * metrics[3]])


def laplacian(field, factors, second):
    total = factors[0] * jnp.einsum("qr,fcre->fcqe", second[0], field, precision=highest)
    total = total + factors[1] * jnp.einsum("qr,fcre->fcqe", second[1], field, precision=highest)
    total = total + factors[2] * jnp.einsum("qr,fcre->fcqe", second[2], field, precision=highest)
    return total


def reference(velocity, metrics, connect, send_list, recv_slot):
    float_tables, edge_nodes = spectral_tables(COEF)
    along_r, along_s, second, scatter_edge, basis, inverse, z_derivative, shifts, plane_derivative = float_tables
    element_total = velocity.shape[3]
    blocks = velocity.reshape(3, COEF, 81, N_MESH, E_DEV).transpose(3, 0, 1, 2, 4)
    metric_blocks = metrics.reshape(4, N_MESH, E_DEV).transpose(1, 0, 2)

    def advect(paired):
        vel_block, met_block = paired
        grad_r = jnp.einsum("qr,fcre->fcqe", along_r, vel_block, precision=highest)
        grad_s = jnp.einsum("qr,fcre->fcqe", along_s, vel_block, precision=highest)
        grad_x = met_block[0] * grad_r + met_block[2] * grad_s
        grad_y = met_block[1] * grad_r + met_block[3] * grad_s
        grad_z = jnp.einsum("cd,fdqe->fcqe", z_derivative, vel_block, precision=highest)
        stacked = jnp.concatenate([vel_block, grad_x, grad_y, grad_z], axis=0)
        physical = jnp.einsum("pc,fcqe->fpqe", basis, stacked, precision=highest)
        term = physical[0] * physical[3:6] + physical[1] * physical[6:9] + physical[2] * physical[9:12]
        return jnp.einsum("cp,fpqe->fcqe", inverse, term, precision=highest)

    advected = lax.map(advect, (blocks, metric_blocks))
    advection = advected.transpose(1, 2, 3, 0, 4).reshape(3, COEF, 81, element_total)

    factors = element_factors(metrics)
    precond = shifts[:, None] + spectral_bound * (factors[0] + factors[2])[None, :] + penalty_weight
    part_of = jnp.arange(element_total, dtype=jnp.int32) // E_DEV
    has_local = (connect >= 0).astype(jnp.float32)
    picks = jnp.clip(connect, 0, element_total - 1)
    width_cols = send_list.shape[1]
    lower_cols = recv_slot[:, 0]
    upper_cols = recv_slot[:, 1]
    lower_source = part_of - 1
    lower_valid = (lower_source >= 0).astype(jnp.float32)
    lower_clip = jnp.clip(lower_source, 0, N_MESH - 1)
    lower_sender = lower_clip * E_DEV + send_list[2 * lower_clip + 1, jnp.clip(lower_cols, 0, width_cols - 1)]
    upper_source = part_of + 1
    upper_valid = (upper_source < N_MESH).astype(jnp.float32)
    upper_clip = jnp.clip(upper_source, 0, N_MESH - 1)
    upper_sender = upper_clip * E_DEV + send_list[2 * upper_clip, jnp.clip(upper_cols, 0, width_cols - 1)]
    opposite = [2, 3, 0, 1]

    def operator(field):
        traces = field[:, :, edge_nodes, :]
        nearby = []
        for edge_index in range(4):
            nearby.append(jnp.take(traces[:, :, opposite[edge_index]], picks[:, edge_index], axis=-1) * has_local[:, edge_index])
        nearby[0] = jnp.where(lower_cols >= 0, jnp.take(traces[:, :, 2], lower_sender, axis=-1) * lower_valid, nearby[0])
        nearby[2] = jnp.where(upper_cols >= 0, jnp.take(traces[:, :, 0], upper_sender, axis=-1) * upper_valid, nearby[2])
        neighbours = jnp.stack(nearby, axis=2)
        differences = (traces - neighbours).reshape(field.shape[0], field.shape[1], 36, field.shape[3])
        penalty = jnp.einsum("qt,fcte->fcqe", scatter_edge, differences, precision=highest)
        return shifts[:, None, None] * field - laplacian(field, factors, second) + penalty_weight * penalty

    right_side = helm_shift * (velocity - time_step * advection)
    state = velocity
    for sweep in range(ITERS):
        applied = operator(state)
        state = state + relaxation * (right_side - applied) / precond[:, None, :]
    return state, advection
```

```python
import jax
import jax.numpy as jnp
import numpy as np
from jax import lax
from jax.experimental import pallas as pl
from jax.experimental.pallas import tpu as pltpu
from jax.sharding import PartitionSpec as P

COEF = 128
ITERS = 2


highest = lax.Precision.HIGHEST
helm_shift = 4.0
penalty_weight = 200.0
spectral_bound = 400.0
relaxation = 0.8
time_step = 0.02
wave_scale = 0.125
gll_interior = [
    -0.8997579954114602,
    -0.6771862795107377,
    -0.3631174638261782,
    0.0,
    0.3631174638261782,
    0.6771862795107377,
    0.8997579954114602,
]


def shifted(block, axis, distance):
    devices = range(lax.axis_size(axis))
    route = [(i - distance, i) for i in devices if i - distance in devices]
    return lax.ppermute(block, axis, route)


def legendre_value(point, degree):
    previous = 1.0
    current = point
    for order_index in range(1, degree):
        following = ((2 * order_index + 1) * point * current - order_index * previous) / (
            order_index + 1
        )
        previous = current
        current = following
    return current


def spectral_tables(coef_count):
    poly_order = 8
    node_count = poly_order + 1
    points = np.array([-1.0] + gll_interior + [1.0])
    values = np.array([legendre_value(points[node], poly_order) for node in range(node_count)])
    derivative = np.zeros((node_count, node_count))
    for row_index in range(node_count):
        for col_index in range(node_count):
            if row_index != col_index:
                derivative[row_index, col_index] = values[row_index] / (
                    values[col_index] * (points[row_index] - points[col_index])
                )
    derivative[0, 0] = -poly_order * (poly_order + 1) / 4.0
    derivative[poly_order, poly_order] = poly_order * (poly_order + 1) / 4.0
    identity = np.eye(node_count)
    along_r = np.kron(identity, derivative)
    along_s = np.kron(derivative, identity)
    second = np.stack([along_r @ along_r, along_r @ along_s, along_s @ along_s])
    line_nodes = np.arange(node_count)
    edge_nodes = np.stack(
        [
            line_nodes,
            line_nodes * node_count + poly_order,
            poly_order * node_count + line_nodes,
            line_nodes * node_count,
        ]
    )
    scatter_edge = np.zeros((node_count * node_count, 4 * node_count))
    for edge_index in range(4):
        scatter_edge[edge_nodes[edge_index], edge_index * node_count + line_nodes] = 1.0
    planes = np.arange(coef_count) * 2.0 * np.pi / coef_count
    half_count = coef_count // 2
    wavenumber = np.zeros(coef_count)
    basis = np.zeros((coef_count, coef_count))
    z_derivative = np.zeros((coef_count, coef_count))
    basis[:, 0] = 1.0
    basis[:, 1] = np.cos(half_count * planes)
    wavenumber[1] = half_count
    for mode_number in range(1, half_count):
        basis[:, 2 * mode_number] = np.cos(mode_number * planes)
        basis[:, 2 * mode_number + 1] = np.sin(mode_number * planes)
        wavenumber[2 * mode_number] = mode_number
        wavenumber[2 * mode_number + 1] = mode_number
        z_derivative[2 * mode_number, 2 * mode_number + 1] = wave_scale * mode_number
        z_derivative[2 * mode_number + 1, 2 * mode_number] = -wave_scale * mode_number
    norms = np.full(coef_count, coef_count / 2.0)
    norms[0] = coef_count
    norms[1] = coef_count
    inverse = basis.T / norms[:, None]
    shifts = helm_shift + (wave_scale * wavenumber) ** 2
    plane_derivative = basis @ z_derivative @ inverse
    return (derivative, second, scatter_edge, basis, inverse, z_derivative, shifts, edge_nodes)


def dot(left, right, left_dim, right_dim):
    return lax.dot_general(
        left,
        right,
        (((left_dim,), (right_dim,)), ((), ())),
        precision=highest,
        preferred_element_type=jnp.float32,
    )


def advection_kernel(deriv, moved, forward, backward, metrics, out, physical, grad_z):
    peers, fields, blocks, coefs, lanes = moved.shape
    elems = physical.shape[2]
    derivative = spectral_tables(COEF)[0]
    for field in range(fields):
        for block in range(blocks):
            values = dot(moved[:, field, block].reshape(COEF, lanes), forward[...], 0, 0)
            rows = pl.ds(block * 8, 8)
            physical[field, rows] = values[:, :COEF].reshape(8, elems, COEF)
            grad_z[field, rows] = values[:, COEF:].reshape(8, elems, COEF)

    def line(i, carry):
        weights = [deriv[i, k] for k in range(9)]
        speeds = []
        for j in range(9):
            u = physical[0, 9 * i + j]
            v = physical[1, 9 * i + j]
            speeds.append(
                (u * metrics[0] + v * metrics[1], u * metrics[2] + v * metrics[3])
            )
        for field in range(fields):
            along = [physical[field, 9 * i + j] for j in range(9)]
            for j in range(9):
                grad_r = sum(float(derivative[j, k]) * along[k] for k in range(9))
                grad_s = sum(weights[k] * physical[field, 9 * k + j] for k in range(9))
                node = 9 * i + j
                grad_z[field, node] = (
                    speeds[j][0] * grad_r
                    + speeds[j][1] * grad_s
                    + physical[2, node] * grad_z[field, node]
                )
        return carry

    lax.fori_loop(0, 9, line, 0)
    for field in range(fields):
        for block in range(blocks):
            term = grad_z[field, pl.ds(block * 8, 8)].reshape(lanes, COEF)
            out[:, field, block] = dot(backward[...], term, 1, 1).reshape(peers, coefs, lanes)


def advect(moved, metrics, derivative, forward, backward):
    peers, fields, blocks, coefs, lanes = moved.shape
    elems = lanes // 8
    space = pltpu.VMEM
    return pl.pallas_call(
        advection_kernel,
        out_shape=jax.ShapeDtypeStruct(moved.shape, jnp.float32),
        in_specs=[pl.BlockSpec(memory_space=pltpu.SMEM)]
        + [pl.BlockSpec(memory_space=space)] * 4,
        out_specs=pl.BlockSpec(memory_space=space),
        scratch_shapes=[
            pltpu.VMEM((fields, blocks * 8, elems, COEF), jnp.float32),
            pltpu.VMEM((fields, blocks * 8, elems, COEF), jnp.float32),
        ],
        compiler_params=pltpu.CompilerParams(vmem_limit_bytes=48 * 1024 * 1024),
    )(derivative, moved, forward, backward, metrics)


def element_factors(metrics):
    return jnp.stack(
        [
            metrics[0] * metrics[0] + metrics[1] * metrics[1],
            2.0 * (metrics[0] * metrics[2] + metrics[1] * metrics[3]),
            metrics[2] * metrics[2] + metrics[3] * metrics[3],
        ]
    )


def body(velocity, metrics, connect, send_list, recv_slot):
    derivative, second, scatter_edge, basis, inverse, z_derivative, shifts, edge_nodes = (
        spectral_tables(COEF)
    )
    as_f32 = lambda table: jnp.asarray(table, dtype=jnp.float32)
    peers = lax.axis_size("modes")
    mode_index = lax.axis_index("modes")
    mesh_index = lax.axis_index("mesh")
    fields, coefs, nodes, element_count = velocity.shape
    elems = element_count // peers
    blocks = -(-nodes // 8)
    lanes = 8 * elems
    shifts_here = lax.dynamic_slice_in_dim(as_f32(shifts), mode_index * coefs, coefs)

    padded = jnp.pad(velocity, ((0, 0), (0, 0), (0, blocks * 8 - nodes), (0, 0)))
    packed = (
        padded.reshape(fields, coefs, blocks, 8, peers, elems)
        .transpose(4, 0, 2, 1, 3, 5)
        .reshape(peers, fields, blocks, coefs, lanes)
    )
    moved = lax.all_to_all(packed, "modes", split_axis=0, concat_axis=0, tiled=True)
    metrics_here = lax.dynamic_slice_in_dim(metrics, mode_index * elems, elems, axis=1)
    metric_tiles = jnp.broadcast_to(metrics_here[:, :, None], (4, elems, COEF))
    forward = as_f32(np.concatenate([basis.T, (basis @ z_derivative).T], axis=1))
    spectral = advect(moved, metric_tiles, as_f32(derivative), forward, as_f32(inverse))
    returned = lax.all_to_all(spectral, "modes", split_axis=0, concat_axis=0, tiled=True)
    advection = (
        returned.reshape(peers, fields, blocks, coefs, 8, elems)
        .transpose(1, 3, 2, 4, 0, 5)
        .reshape(fields, coefs, blocks * 8, element_count)[:, :, :nodes]
    )

    factors = element_factors(metrics)
    precond = (
        shifts_here[:, None] + spectral_bound * (factors[0] + factors[2])[None, :] + penalty_weight
    )
    ids = jnp.arange(element_count)
    picks = connect - mesh_index * element_count
    lower_cols = recv_slot[:, 0]
    upper_cols = recv_slot[:, 1]
    slots = jnp.arange(send_list.shape[1])
    local = [ids[:, None] == picks[None, :, k] for k in range(4)]
    local[0] = local[0] & (lower_cols < 0)
    local[2] = local[2] & (upper_cols < 0)
    local = [one.astype(jnp.float32) for one in local]
    lower = (slots[:, None] == lower_cols[None, :]).astype(jnp.float32)
    upper = (slots[:, None] == upper_cols[None, :]).astype(jnp.float32)
    send_down = (ids[:, None] == send_list[0][None, :]).astype(jnp.float32)
    send_up = (ids[:, None] == send_list[1][None, :]).astype(jnp.float32)
    opposite = [2, 3, 0, 1]
    stacked_second = as_f32(second.reshape(3 * nodes, nodes))
    scatter = as_f32(scatter_edge)

    def pick(trace, matrix):
        return jnp.einsum("fcte,es->fcts", trace, matrix, precision=highest)

    def operator(field):
        traces = [field[:, :, edge_nodes[k], :] for k in range(4)]
        from_lower = shifted(pick(traces[2], send_up), "mesh", 1)
        from_upper = shifted(pick(traces[0], send_down), "mesh", -1)
        nearby = [pick(traces[opposite[k]], local[k]) for k in range(4)]
        nearby[0] = nearby[0] + pick(from_lower, lower)
        nearby[2] = nearby[2] + pick(from_upper, upper)
        differences = jnp.concatenate(
            [traces[k] - nearby[k] for k in range(4)], axis=2
        )
        penalty = jnp.einsum("qt,fcte->fcqe", scatter, differences, precision=highest)
        parts = jnp.einsum("qr,fcre->fcqe", stacked_second, field, precision=highest)
        lap = (
            factors[0] * parts[:, :, :nodes]
            + factors[1] * parts[:, :, nodes : 2 * nodes]
            + factors[2] * parts[:, :, 2 * nodes :]
        )
        return shifts_here[:, None, None] * field - lap + penalty_weight * penalty

    applied = operator(velocity)
    right_side = helm_shift * (velocity - time_step * advection)
    state = velocity
    for sweep in range(ITERS):
        state = state + relaxation * (right_side - applied) / precond[:, None, :]
        if sweep + 1 < ITERS:
            applied = operator(state)
    return (state, advection)


def solution(mesh):
    return jax.shard_map(
        body,
        mesh=mesh,
        in_specs=(
            P(None, "modes", None, "mesh"),
            P(None, "mesh"),
            P("mesh", None),
            P("mesh", None),
            P("mesh", None),
        ),
        out_specs=(P(None, "modes", None, "mesh"), P(None, "modes", None, "mesh")),
        check_vma=False,
    )
```
